256 devices in a mesh: orb: 16 (over y, x), aux: 16 (over z, core).
Axes of the slice: x: 4, y: 4, z: 8, core: 2. Of those that a mesh axis runs over, the one named last changes fastest.
Arguments:
- b_rows: bfloat16 [4096, 128, 8, 128], P('aux', 'orb'), may hold values from -6 to 6
- col_blocks: int32 [16, 8], P('orb'), may hold values from 0 to 15, all different within a row
- g_occ: bfloat16 [2, 128, 128], P(None, 'orb'), may hold values from -0.5 to 0.5
- occ_live: int32 [2, 16, 16], replicated, may hold values 0 or 1
- g_virt: bfloat16 [2, 16, 128, 128], P(None, 'orb', 'aux'), may hold values from -0.5 to 0.5
- tau_weight: float32 [2], replicated, may hold values from 0.5 to 2
Outputs:
- chi: float32 [256, 4096], P('orb', 'aux')
The draws below stay inside these ranges and needn't reach their ends.
Inputs may be any that keep to these rules, and one draw needn't show every extreme that they name: `col_blocks`: each row group lists 8 different column blocks, and every column block is listed by some row group.
All inputs are finite; a program needn't handle non-finite values.
Results may differ from the reference program's by a relative error of at most 0.0041.
Values may be sent and summed in bfloat16 or wider, within the bound.
A program may use at most 128 MiB of HBM per device.

```python
import math
import jax
import jax.numpy as jnp
from jax import lax

AUX_DEV = 256
TILE = 128
RD = 8
TAU = 2
AUX = 4096
GROUPS = 16
NROW = 128
NBLK = 16
K = 8


def touch_ends(drawn, own_key, least, high):
    dims = drawn.shape
    place = [jax.random.randint(jax.random.fold_in(own_key, axis), (), 0, dims[axis]) for axis in range(len(dims))]
    drawn = drawn.at[tuple(place)].set(least)
    longest = dims.index(max(dims))
    place[longest] = (place[longest] + 1) % dims[longest]
    return drawn.at[tuple(place)].set(high)


def level_of(own_key, shape, cuts, low, largest):
    level = 1.0
    for axis_at, parts in cuts:
        steps = jax.random.uniform(jax.random.fold_in(jax.random.fold_in(own_key, 6), axis_at), (parts,), jnp.float32, low / len(cuts), largest / len(cuts))
        level = level * jnp.repeat(jnp.exp(steps), shape[axis_at] // parts).reshape((-1,) + (1,) * (len(shape) - 1 - axis_at))
    return level


def distinct(key, rows, amount, top, lift):
    order = jax.random.permutation(jax.random.fold_in(key, 1), amount)
    boost = order
    for power in range(3):
        boost = boost * boost // amount
    boost = boost * lift // amount
    tickets = jax.random.randint(jax.random.fold_in(key, 2), (rows, amount), 0, 4096) + boost
    sure = jax.random.permutation(jax.random.fold_in(key, 3), rows)[jnp.arange(amount) % rows]
    tickets = jnp.where(jnp.arange(rows)[:, None] == sure[None, :], 1 << 14, tickets)
    priority = tickets * amount + jnp.arange(amount)
    return lax.top_k(priority.astype(jnp.int32), top)[1].astype(jnp.int32)


def centred(stream_key, shape, deviation, reach, pieces=(), kind=jnp.bfloat16):
    values = jax.random.normal(stream_key, shape, jnp.float32) * deviation
    if len(pieces) > 0:
        values = level_of(stream_key, shape, pieces, -0.22, 0.18) * values
    return jnp.clip(values, min=-reach, max=reach).astype(kind)


def setup_inputs(seed: int = 0) -> dict:
    seeds = jax.random.split(jax.random.key(seed), 7)
    return {
        "b_rows": centred(seeds[0], (AUX, NROW, K, TILE), 1.0, 6.0, ((0, 16), (1, 16))),
        "col_blocks": distinct(seeds[1], GROUPS, NBLK, K, 8192),
        "g_occ": centred(seeds[2], (TAU, NROW, NROW), NROW ** -0.5, 0.5, ((1, 16),)),
        "occ_live": touch_ends((jax.random.randint(seeds[3], (TAU, GROUPS, GROUPS), 0, 4) < 3).astype(jnp.int32), jax.random.fold_in(seeds[3], 1), 0, 1),
        "g_virt": centred(seeds[4], (TAU, NBLK, TILE, TILE), TILE ** -0.5, 0.5, ((1, 16), (2, 16))),
        "tau_weight": jnp.clip(jnp.exp(jax.random.uniform(seeds[5], (TAU,), jnp.float32, math.log(0.5), math.log(2.0))), 0.5, 2.0),
    }


def reference(b_rows, col_blocks, g_occ, occ_live, g_virt, tau_weight):
    live_mask = jnp.repeat(jnp.repeat(occ_live, RD, axis=1), RD, axis=2).astype(jnp.bfloat16)
    occ_masked = g_occ * live_mask
    blocks = jnp.arange(NBLK, dtype=jnp.int32)
    scale = 1.0 / math.sqrt(NROW * TILE * NBLK)

    def one_aux(aux_rows):
        grouped = aux_rows.reshape(AUX_DEV, GROUPS, RD, K, TILE).astype(jnp.float32)

        def one_column(total, column):
            chosen = (col_blocks == column).astype(jnp.float32)
            col_dense = jnp.einsum('pgrkc,gk->pgrc', grouped, chosen).reshape(AUX_DEV, NROW, TILE).astype(jnp.bfloat16)
            for moment in range(TAU):
                virt_block = g_virt[moment][column]
                virt_prod = jnp.dot(col_dense.reshape(AUX_DEV * NROW, TILE), virt_block, preferred_element_type=jnp.float32)
                virt_prod = virt_prod.astype(jnp.bfloat16).reshape(AUX_DEV, NROW, TILE)
                occ_prod = jnp.einsum('mn,qnc->qmc', occ_masked[moment].astype(jnp.float32), col_dense.astype(jnp.float32)).astype(jnp.bfloat16)
                term = jnp.einsum('pmc,qmc->qp', virt_prod.astype(jnp.float32), occ_prod.astype(jnp.float32))
                total = total + tau_weight[moment] * term
            return (total, None)
        total, unused = lax.scan(one_column, jnp.zeros((AUX_DEV, AUX_DEV), jnp.float32), blocks)
        return total * scale
    per_aux = lax.map(one_aux, b_rows.reshape(AUX // AUX_DEV, AUX_DEV, NROW, K, TILE))
    return jnp.transpose(per_aux, (1, 0, 2)).reshape(AUX_DEV, AUX)
```

```python
import functools
import math

import jax
import jax.numpy as jnp
from jax import lax
from jax.experimental import pallas as pl
from jax.experimental.pallas import tpu as pltpu
from jax.sharding import PartitionSpec as P

MESH = pl.DeviceIdType.MESH
F32 = jnp.float32
BF16 = jnp.bfloat16
CHUNK = 32


def kernel(
    orb,
    aux,
    side,
    scale,
    col_ref,
    live_ref,
    tau_ref,
    occ_ref,
    gv_ref,
    b_ref,
    out_ref,
    stage,
    send,
    recv,
    virt,
    occp,
    kron,
    select,
    occ_mine,
    occ_all,
    gv_mine,
    gv_all,
    gv_both,
    total,
    part,
    shares,
    stage_sem,
    own_sem,
    send_sem,
    recv_sem,
    small_send,
    small_recv,
    share_send,
    share_recv,
):
    me = lax.axis_index("orb")
    my_aux = lax.axis_index("aux")
    chunks = send.shape[0]
    rows = occ_ref.shape[1]
    total_rows = orb * rows
    width = occ_ref.shape[2]
    slots = col_ref.shape[1]
    my_y, my_x = me // side, me % side

    def orb_peer(step):
        step_y, step_x = step // side, step % side
        return lax.rem(my_y + step_y, side) * side + lax.rem(my_x + step_x, side)

    def aux_peer(step):
        return lax.rem(my_aux + step, aux)

    def load(chunk):
        slot = lax.rem(chunk, 2)
        return pltpu.make_async_copy(
            b_ref.at[pl.ds(chunk * CHUNK, CHUNK)], stage.at[slot], stage_sem.at[slot]
        )

    load(0).start()
    load(1).start()
    barrier = pltpu.get_barrier_semaphore()
    for step in range(1, orb):
        pl.semaphore_signal(
            barrier, inc=1, device_id={"orb": orb_peer(step)}, device_id_type=MESH
        )
    for step in range(1, aux):
        pl.semaphore_signal(
            barrier, inc=1, device_id={"aux": aux_peer(step)}, device_id_type=MESH
        )

    lane = lax.broadcasted_iota(jnp.int32, (16 * orb, 128), 1)
    row = lax.broadcasted_iota(jnp.int32, (16 * orb, 128), 0)
    listed = jnp.zeros((16 * orb, 128), jnp.int32)
    for k in range(slots):
        listed = jnp.where(lane % slots == k, col_ref[0, k], listed)
    select[...] = jnp.where(
        (listed == row // 16) & (row % 16 == lane // slots), 1.0, 0.0
    ).astype(BF16)

    lane = lax.broadcasted_iota(jnp.int32, (rows, width), 1)
    for t in range(2):
        live = jnp.zeros((rows, width), jnp.int32)
        for group in range(orb):
            live = jnp.where(lane // rows == group, live_ref[t, me, group], live)
        occ_mine[t] = (occ_ref[t].astype(F32) * live.astype(F32)).astype(BF16)
        gv_mine[t] = gv_ref[t, 0]
    occ_all[me] = occ_mine[...]
    gv_all[my_aux] = gv_mine[...]

    def pack(chunk):
        slot = lax.rem(chunk, 2)
        load(chunk).wait()
        for half in range(CHUNK // 16):
            for pair in range(rows // 2):
                block = [
                    stage[slot, pl.ds(16 * half, 16), 2 * pair + r].reshape(128, width)
                    for r in range(2)
                ]
                picked = jnp.dot(
                    select[...],
                    jnp.concatenate(block, axis=1),
                    preferred_element_type=F32,
                ).reshape(orb, 2, 8, 2 * width)
                picked = jnp.concatenate(
                    [picked[..., :width], picked[..., width:]], axis=2
                )
                send[chunk, :, pl.ds(2 * half, 2), pl.ds(16 * pair, 16), :] = (
                    picked.astype(BF16)
                )

        @pl.when(chunk + 2 < chunks)
        def _():
            load(chunk + 2).start()

    def own(chunk):
        return pltpu.make_async_copy(
            send.at[chunk, me], recv.at[chunk, :, me], own_sem.at[chunk]
        )

    def start(chunk):
        for step in range(1, orb):
            peer = orb_peer(step)
            pltpu.make_async_remote_copy(
                src_ref=send.at[chunk, peer],
                dst_ref=recv.at[chunk, :, me],
                send_sem=send_sem.at[chunk],
                recv_sem=recv_sem.at[chunk],
                device_id={"orb": peer},
                device_id_type=MESH,
            ).start()
        own(chunk).start()

    pack(0)
    pl.semaphore_wait(barrier, orb + aux - 2)
    start(0)
    for step in range(1, orb):
        pltpu.make_async_remote_copy(
            src_ref=occ_mine,
            dst_ref=occ_all.at[me],
            send_sem=small_send.at[0],
            recv_sem=small_recv.at[0],
            device_id={"orb": orb_peer(step)},
            device_id_type=MESH,
        ).start()
    for step in range(1, aux):
        pltpu.make_async_remote_copy(
            src_ref=gv_mine,
            dst_ref=gv_all.at[my_aux],
            send_sem=small_send.at[1],
            recv_sem=small_recv.at[1],
            device_id={"aux": aux_peer(step)},
            device_id_type=MESH,
        ).start()

    def pack_and_start(chunk, carry):
        pack(chunk)
        start(chunk)
        return carry

    lax.fori_loop(1, chunks, pack_and_start, 0)

    def settle(ref, sem):
        pltpu.make_async_copy(ref, ref, sem).wait()

    settle(occ_all.at[pl.ds(0, orb - 1)], small_recv.at[0])
    settle(gv_all.at[pl.ds(0, aux - 1)], small_recv.at[1])

    for t in range(2):
        gv_both[:, pl.ds(t * width, width)] = gv_all[:, t].reshape(width, width)

    deep = 8 * total_rows
    spread = (
        lax.broadcasted_iota(jnp.int32, (total_rows, deep), 1) // 8
        == lax.broadcasted_iota(jnp.int32, (total_rows, deep), 0)
    )
    spread = jnp.where(spread, 1.0, 0.0).astype(BF16)
    same = (
        lax.broadcasted_iota(jnp.int32, (16, 8, deep), 2) % 8
        == lax.broadcasted_iota(jnp.int32, (16, 8, deep), 1)
    )
    for t in range(2):

        def expand(pair, carry, t=t):
            two = occ_all[pl.ds(2 * pair, 2), t].reshape(2 * rows, width)
            wide = jnp.dot(two, spread, preferred_element_type=F32)
            wide = jnp.broadcast_to(wide[:, None, :], (16, 8, deep))
            wide = jnp.where(same, wide, 0.0).astype(BF16).reshape(128, deep)
            kron[pl.ds(pl.multiple_of((t * orb + 2 * pair) * 64, 128), 128), :] = wide
            return carry

        lax.fori_loop(0, orb // 2, expand, 0)

    def consume(chunk, carry):
        own(chunk).wait()
        settle(send.at[chunk, pl.ds(0, orb - 1)], recv_sem.at[chunk])
        for half in range(CHUNK // 16):
            first = chunk * CHUNK + 16 * half
            two = [recv[chunk, 2 * half + i].reshape(deep, width) for i in range(2)]
            place = pl.ds(pl.multiple_of(first, 16), 16)
            product = [
                jnp.dot(rows8, gv_both[...], preferred_element_type=F32).reshape(
                    total_rows, 8, 2 * width
                )
                for rows8 in two
            ]
            product = jnp.concatenate(product, axis=1).astype(BF16)
            virt[0, :, place, :] = product[..., :width]
            virt[1, :, place, :] = product[..., width:]
            both = jnp.concatenate(two, axis=1)
            for t in range(2):
                mixed = jnp.dot(
                    kron[pl.ds(t * deep, deep), :], both, preferred_element_type=F32
                ).reshape(total_rows, 8, 2 * width)
                mixed = jnp.concatenate([mixed[..., :width], mixed[..., width:]], axis=1)
                occp[t, :, place, :] = mixed.astype(BF16)
        return carry

    lax.fori_loop(0, chunks, consume, 0)

    many = 4
    for t in range(2):
        total[...] = jnp.zeros_like(total)

        def contract(block, carry, t=t):
            left = jnp.concatenate([occp[t, many * block + i] for i in range(many)], axis=1)
            right = jnp.concatenate([virt[t, many * block + i] for i in range(many)], axis=1)
            total[...] += lax.dot_general(
                left, right, (((1,), (1,)), ((), ())), preferred_element_type=F32
            )
            return carry

        lax.fori_loop(0, total_rows // many, contract, 0)
        term = (total[...] * tau_ref[t]).reshape(part.shape)
        part[...] = term if t == 0 else (part[...] + term) * scale

    for step in range(1, orb):
        peer = orb_peer(step)
        pltpu.make_async_remote_copy(
            src_ref=part.at[peer],
            dst_ref=shares.at[me],
            send_sem=share_send,
            recv_sem=share_recv,
            device_id={"orb": peer},
            device_id_type=MESH,
        ).start()
    shares[me] = part[me]
    settle(shares.at[pl.ds(0, orb - 1)], share_recv)
    whole = shares[0]
    for group in range(1, orb):
        whole = whole + shares[group]
    out_ref[...] = whole

    settle(shares.at[pl.ds(0, orb - 1)], share_send)
    settle(occ_all.at[pl.ds(0, orb - 1)], small_send.at[0])
    settle(gv_all.at[pl.ds(0, aux - 1)], small_send.at[1])

    def finish(chunk, carry):
        settle(send.at[chunk, pl.ds(0, orb - 1)], send_sem.at[chunk])
        return carry

    lax.fori_loop(0, chunks, finish, 0)


def on_device(b_rows, col_blocks, g_occ, occ_live, g_virt, tau_weight):
    orb, aux = lax.axis_size("orb"), lax.axis_size("aux")
    aux_dev, rows, slots, width = b_rows.shape
    chunks = aux_dev // CHUNK
    total_rows = orb * rows
    deep = 8 * total_rows
    scale = 1.0 / math.sqrt(total_rows * width * orb)
    smem = pl.BlockSpec(memory_space=pltpu.SMEM)
    vmem = pl.BlockSpec(memory_space=pltpu.VMEM)
    share = aux_dev // orb
    dma = pltpu.SemaphoreType.DMA
    return pl.pallas_call(
        functools.partial(kernel, orb, aux, math.isqrt(orb), scale),
        out_shape=jax.ShapeDtypeStruct((share, aux_dev), F32),
        in_specs=[smem, smem, smem, vmem, vmem, pl.BlockSpec(memory_space=pl.ANY)],
        out_specs=vmem,
        scratch_shapes=[
            pltpu.VMEM((2, CHUNK, rows, slots, width), BF16),
            pltpu.VMEM((chunks, orb, CHUNK // 8, 8 * rows, width), BF16),
            pltpu.VMEM((chunks, CHUNK // 8, orb, 8 * rows, width), BF16),
            pltpu.VMEM((2, total_rows, aux_dev, width), BF16),
            pltpu.VMEM((2, total_rows, aux_dev, width), BF16),
            pltpu.VMEM((2 * deep, deep), BF16),
            pltpu.VMEM((16 * orb, 128), BF16),
            pltpu.VMEM((2, rows, width), BF16),
            pltpu.VMEM((orb, 2, rows, width), BF16),
            pltpu.VMEM((2, rows, width), BF16),
            pltpu.VMEM((aux, 2, rows, width), BF16),
            pltpu.VMEM((width, 2 * width), BF16),
            pltpu.VMEM((aux_dev, aux_dev), F32),
            pltpu.VMEM((orb, share, aux_dev), F32),
            pltpu.VMEM((orb, share, aux_dev), F32),
            dma((2,)),
            dma((chunks,)),
            dma((chunks,)),
            dma((chunks,)),
            dma((2,)),
            dma((2,)),
            dma(()),
            dma(()),
        ],
        compiler_params=pltpu.CompilerParams(
            collective_id=0, has_side_effects=True, vmem_limit_bytes=61 * 1024 * 1024
        ),
    )(col_blocks, occ_live, tau_weight, g_occ, g_virt, b_rows)


def solution(mesh):
    in_specs = (
        P("aux", "orb", None, None),
        P("orb", None),
        P(None, "orb", None),
        P(),
        P(None, "orb", "aux", None),
        P(),
    )
    out_specs = P("orb", "aux")
    return jax.shard_map(
        on_device, mesh=mesh, in_specs=in_specs, out_specs=out_specs, check_vma=False
    )
```

```python
import functools
import math

import jax
import jax.numpy as jnp
from jax import lax
from jax.experimental import pallas as pl
from jax.experimental.pallas import tpu as pltpu
from jax.sharding import PartitionSpec as P

MESH = pl.DeviceIdType.MESH
F32 = jnp.float32
BF16 = jnp.bfloat16
CHUNK = 16


def kernel(
    orb,
    aux,
    side,
    scale,
    col_ref,
    live_ref,
    tau_ref,
    occ_ref,
    gv_ref,
    b_ref,
    out_ref,
    stage,
    send,
    recv,
    virt,
    occp,
    kron,
    select,
    occ_mine,
    occ_all,
    gv_mine,
    gv_all,
    gv_both,
    total,
    part,
    shares,
    stage_sem,
    own_sem,
    send_sem,
    recv_sem,
    small_send,
    small_recv,
    share_send,
    share_recv,
):
    me = lax.axis_index("orb")
    my_aux = lax.axis_index("aux")
    chunks = send.shape[0]
    rows = occ_ref.shape[1]
    total_rows = orb * rows
    width = occ_ref.shape[2]
    slots = col_ref.shape[1]
    my_y, my_x = me // side, me % side

    def orb_peer(step):
        step_y, step_x = step // side, step % side
        return lax.rem(my_y + step_y, side) * side + lax.rem(my_x + step_x, side)

    def aux_peer(step):
        return lax.rem(my_aux + step, aux)

    def load(chunk):
        slot = lax.rem(chunk, 2)
        return pltpu.make_async_copy(
            b_ref.at[pl.ds(chunk * CHUNK, CHUNK)], stage.at[slot], stage_sem.at[slot]
        )

    load(0).start()
    load(1).start()
    barrier = pltpu.get_barrier_semaphore()
    for step in range(1, orb):
        pl.semaphore_signal(
            barrier, inc=1, device_id={"orb": orb_peer(step)}, device_id_type=MESH
        )
    for step in range(1, aux):
        pl.semaphore_signal(
            barrier, inc=1, device_id={"aux": aux_peer(step)}, device_id_type=MESH
        )

    lane = lax.broadcasted_iota(jnp.int32, (16 * orb, 128), 1)
    row = lax.broadcasted_iota(jnp.int32, (16 * orb, 128), 0)
    listed = jnp.zeros((16 * orb, 128), jnp.int32)
    for k in range(slots):
        listed = jnp.where(lane % slots == k, col_ref[0, k], listed)
    select[...] = jnp.where(
        (listed == row // 16) & (row % 16 == lane // slots), 1.0, 0.0
    ).astype(BF16)

    lane = lax.broadcasted_iota(jnp.int32, (rows, width), 1)
    for t in range(2):
        live = jnp.zeros((rows, width), jnp.int32)
        for group in range(orb):
            live = jnp.where(lane // rows == group, live_ref[t, me, group], live)
        occ_mine[t] = (occ_ref[t].astype(F32) * live.astype(F32)).astype(BF16)
        gv_mine[t] = gv_ref[t, 0]
    occ_all[me] = occ_mine[...]
    gv_all[my_aux] = gv_mine[...]

    def pack(chunk):
        slot = lax.rem(chunk, 2)
        load(chunk).wait()
        for half in range(CHUNK // 16):
            for pair in range(rows // 2):
                block = [
                    stage[slot, pl.ds(16 * half, 16), 2 * pair + r].reshape(128, width)
                    for r in range(2)
                ]
                picked = jnp.dot(
                    select[...],
                    jnp.concatenate(block, axis=1),
                    preferred_element_type=F32,
                ).reshape(orb, 2, 8, 2 * width)
                picked = jnp.concatenate(
                    [picked[..., :width], picked[..., width:]], axis=2
                )
                send[chunk, :, pl.ds(2 * half, 2), pl.ds(16 * pair, 16), :] = (
                    picked.astype(BF16)
                )

        @pl.when(chunk + 2 < chunks)
        def _():
            load(chunk + 2).start()

    def own(chunk):
        return pltpu.make_async_copy(
            send.at[chunk, me], recv.at[chunk, :, me], own_sem.at[chunk]
        )

    def start(chunk):
        for step in range(1, orb):
            peer = orb_peer(step)
            pltpu.make_async_remote_copy(
                src_ref=send.at[chunk, peer],
                dst_ref=recv.at[chunk, :, me],
                send_sem=send_sem.at[chunk],
                recv_sem=recv_sem.at[chunk],
                device_id={"orb": peer},
                device_id_type=MESH,
            ).start()
        own(chunk).start()

    pack(0)
    pl.semaphore_wait(barrier, orb + aux - 2)
    start(0)
    for step in range(1, orb):
        pltpu.make_async_remote_copy(
            src_ref=occ_mine,
            dst_ref=occ_all.at[me],
            send_sem=small_send.at[0],
            recv_sem=small_recv.at[0],
            device_id={"orb": orb_peer(step)},
            device_id_type=MESH,
        ).start()
    for step in range(1, aux):
        pltpu.make_async_remote_copy(
            src_ref=gv_mine,
            dst_ref=gv_all.at[my_aux],
            send_sem=small_send.at[1],
            recv_sem=small_recv.at[1],
            device_id={"aux": aux_peer(step)},
            device_id_type=MESH,
        ).start()

    def pack_and_start(chunk, carry):
        pack(chunk)
        start(chunk)
        return carry

    lax.fori_loop(1, chunks, pack_and_start, 0)

    def settle(ref, sem):
        pltpu.make_async_copy(ref, ref, sem).wait()

    settle(occ_all.at[pl.ds(0, orb - 1)], small_recv.at[0])
    settle(gv_all.at[pl.ds(0, aux - 1)], small_recv.at[1])

    for t in range(2):
        gv_both[:, pl.ds(t * width, width)] = gv_all[:, t].reshape(width, width)

    deep = 8 * total_rows
    spread = (
        lax.broadcasted_iota(jnp.int32, (total_rows, deep), 1) // 8
        == lax.broadcasted_iota(jnp.int32, (total_rows, deep), 0)
    )
    spread = jnp.where(spread, 1.0, 0.0).astype(BF16)
    same = (
        lax.broadcasted_iota(jnp.int32, (16, 8, deep), 2) % 8
        == lax.broadcasted_iota(jnp.int32, (16, 8, deep), 1)
    )
    for t in range(2):

        def expand(pair, carry, t=t):
            two = occ_all[pl.ds(2 * pair, 2), t].reshape(2 * rows, width)
            wide = jnp.dot(two, spread, preferred_element_type=F32)
            wide = jnp.broadcast_to(wide[:, None, :], (16, 8, deep))
            wide = jnp.where(same, wide, 0.0).astype(BF16).reshape(128, deep)
            kron[pl.ds(pl.multiple_of((t * orb + 2 * pair) * 64, 128), 128), :] = wide
            return carry

        lax.fori_loop(0, orb // 2, expand, 0)

    def consume(chunk, carry):
        own(chunk).wait()
        settle(send.at[chunk, pl.ds(0, orb - 1)], recv_sem.at[chunk])
        for half in range(CHUNK // 16):
            first = chunk * CHUNK + 16 * half
            two = [recv[chunk, 2 * half + i].reshape(deep, width) for i in range(2)]
            place = pl.ds(pl.multiple_of(first, 16), 16)
            product = [
                jnp.dot(rows8, gv_both[...], preferred_element_type=F32).reshape(
                    total_rows, 8, 2 * width
                )
                for rows8 in two
            ]
            product = jnp.concatenate(product, axis=1).astype(BF16)
            virt[0, :, place, :] = product[..., :width]
            virt[1, :, place, :] = product[..., width:]
            both = jnp.concatenate(two, axis=1)
            for t in range(2):
                mixed = jnp.dot(
                    kron[pl.ds(t * deep, deep), :], both, preferred_element_type=F32
                ).reshape(total_rows, 8, 2 * width)
                mixed = jnp.concatenate([mixed[..., :width], mixed[..., width:]], axis=1)
                occp[t, :, place, :] = mixed.astype(BF16)
        return carry

    lax.fori_loop(0, chunks, consume, 0)

    many = 32
    for t in range(2):
        total[...] = jnp.zeros_like(total)

        def contract(block, carry, t=t):
            left = jnp.concatenate([occp[t, many * block + i] for i in range(many)], axis=1)
            right = jnp.concatenate([virt[t, many * block + i] for i in range(many)], axis=1)
            total[...] += lax.dot_general(
                left, right, (((1,), (1,)), ((), ())), preferred_element_type=F32
            )
            return carry

        lax.fori_loop(0, total_rows // many, contract, 0)
        term = (total[...] * tau_ref[t]).reshape(part.shape)
        part[...] = term if t == 0 else (part[...] + term) * scale

    for step in range(1, orb):
        peer = orb_peer(step)
        pltpu.make_async_remote_copy(
            src_ref=part.at[peer],
            dst_ref=shares.at[me],
            send_sem=share_send,
            recv_sem=share_recv,
            device_id={"orb": peer},
            device_id_type=MESH,
        ).start()
    shares[me] = part[me]
    settle(shares.at[pl.ds(0, orb - 1)], share_recv)
    whole = shares[0]
    for group in range(1, orb):
        whole = whole + shares[group]
    out_ref[...] = whole

    settle(shares.at[pl.ds(0, orb - 1)], share_send)
    settle(occ_all.at[pl.ds(0, orb - 1)], small_send.at[0])
    settle(gv_all.at[pl.ds(0, aux - 1)], small_send.at[1])

    def finish(chunk, carry):
        settle(send.at[chunk, pl.ds(0, orb - 1)], send_sem.at[chunk])
        return carry

    lax.fori_loop(0, chunks, finish, 0)


def on_device(b_rows, col_blocks, g_occ, occ_live, g_virt, tau_weight):
    orb, aux = lax.axis_size("orb"), lax.axis_size("aux")
    aux_dev, rows, slots, width = b_rows.shape
    chunks = aux_dev // CHUNK
    total_rows = orb * rows
    deep = 8 * total_rows
    scale = 1.0 / math.sqrt(total_rows * width * orb)
    smem = pl.BlockSpec(memory_space=pltpu.SMEM)
    vmem = pl.BlockSpec(memory_space=pltpu.VMEM)
    share = aux_dev // orb
    dma = pltpu.SemaphoreType.DMA
    return pl.pallas_call(
        functools.partial(kernel, orb, aux, math.isqrt(orb), scale),
        out_shape=jax.ShapeDtypeStruct((share, aux_dev), F32),
        in_specs=[smem, smem, smem, vmem, vmem, pl.BlockSpec(memory_space=pl.ANY)],
        out_specs=vmem,
        scratch_shapes=[
            pltpu.VMEM((2, CHUNK, rows, slots, width), BF16),
            pltpu.VMEM((chunks, orb, CHUNK // 8, 8 * rows, width), BF16),
            pltpu.VMEM((chunks, CHUNK // 8, orb, 8 * rows, width), BF16),
            pltpu.VMEM((2, total_rows, aux_dev, width), BF16),
            pltpu.VMEM((2, total_rows, aux_dev, width), BF16),
            pltpu.VMEM((2 * deep, deep), BF16),
            pltpu.VMEM((16 * orb, 128), BF16),
            pltpu.VMEM((2, rows, width), BF16),
            pltpu.VMEM((orb, 2, rows, width), BF16),
            pltpu.VMEM((2, rows, width), BF16),
            pltpu.VMEM((aux, 2, rows, width), BF16),
            pltpu.VMEM((width, 2 * width), BF16),
            pltpu.VMEM((aux_dev, aux_dev), F32),
            pltpu.VMEM((orb, share, aux_dev), F32),
            pltpu.VMEM((orb, share, aux_dev), F32),
            dma((2,)),
            dma((chunks,)),
            dma((chunks,)),
            dma((chunks,)),
            dma((2,)),
            dma((2,)),
            dma(()),
            dma(()),
        ],
        compiler_params=pltpu.CompilerParams(
            collective_id=0, has_side_effects=True, vmem_limit_bytes=61 * 1024 * 1024
        ),
    )(col_blocks, occ_live, tau_weight, g_occ, g_virt, b_rows)


def solution(mesh):
    in_specs = (
        P("aux", "orb", None, None),
        P("orb", None),
        P(None, "orb", None),
        P(),
        P(None, "orb", "aux", None),
        P(),
    )
    out_specs = P("orb", "aux")
    return jax.shard_map(
        on_device, mesh=mesh, in_specs=in_specs, out_specs=out_specs, check_vma=False
    )
```

```python
import functools
import math

import jax
import jax.numpy as jnp
from jax import lax
from jax.experimental import pallas as pl
from jax.experimental.pallas import tpu as pltpu
from jax.sharding import PartitionSpec as P

MESH = pl.DeviceIdType.MESH
F32 = jnp.float32
BF16 = jnp.bfloat16
CHUNK = 16
CORES = 2


def kernel(
    orb,
    aux,
    side,
    scale,
    col_ref,
    live_ref,
    tau_ref,
    occ_ref,
    gv_ref,
    b_ref,
    out_ref,
    stage,
    send,
    recv,
    virt,
    occp,
    kron,
    select,
    occ_mine,
    occ_all,
    gv_mine,
    gv_all,
    gv_both,
    total,
    part,
    shares,
    stage_sem,
    own_sem,
    send_sem,
    recv_sem,
    small_send,
    small_recv,
    share_send,
    share_recv,
    pair_sem,
    down_sem,
    up_sem,
):
    me = lax.axis_index("orb")
    my_aux = lax.axis_index("aux")
    planes = aux // CORES
    my_z, my_core = my_aux // CORES, my_aux % CORES
    chunks = send.shape[0]
    rows = occ_ref.shape[1]
    total_rows = orb * rows
    width = occ_ref.shape[2]
    slots = col_ref.shape[1]
    my_y, my_x = me // side, me % side

    def orb_peer(step):
        step_y, step_x = step // side, step % side
        return lax.rem(my_y + step_y, side) * side + lax.rem(my_x + step_x, side)

    def at(z, core):
        return {"aux": z * CORES + core}

    def load(chunk):
        slot = lax.rem(chunk, 2)
        return pltpu.make_async_copy(
            b_ref.at[pl.ds(chunk * CHUNK, CHUNK)], stage.at[slot], stage_sem.at[slot]
        )

    load(0).start()
    load(1).start()
    barrier = pltpu.get_barrier_semaphore()
    for step in range(1, orb):
        pl.semaphore_signal(
            barrier, inc=1, device_id={"orb": orb_peer(step)}, device_id_type=MESH
        )
    for ahead, target in ((my_z < planes - 1, at(my_z + 1, my_core)), (my_core == 0, at(my_z, 1))):

        @pl.when(ahead)
        def _(target=target):
            pl.semaphore_signal(barrier, inc=1, device_id=target, device_id_type=MESH)

    lane = lax.broadcasted_iota(jnp.int32, (16 * orb, 128), 1)
    row = lax.broadcasted_iota(jnp.int32, (16 * orb, 128), 0)
    listed = jnp.zeros((16 * orb, 128), jnp.int32)
    for k in range(slots):
        listed = jnp.where(lane % slots == k, col_ref[0, k], listed)
    select[...] = jnp.where(
        (listed == row // 16) & (row % 16 == lane // slots), 1.0, 0.0
    ).astype(BF16)

    lane = lax.broadcasted_iota(jnp.int32, (rows, width), 1)
    for t in range(2):
        live = jnp.zeros((rows, width), jnp.int32)
        for group in range(orb):
            live = jnp.where(lane // rows == group, live_ref[t, me, group], live)
        occ_mine[t] = (occ_ref[t].astype(F32) * live.astype(F32)).astype(BF16)
        gv_mine[t] = gv_ref[t, 0]
    occ_all[me] = occ_mine[...]
    gv_all[my_core, my_z] = gv_mine[...]

    def pack(chunk):
        slot = lax.rem(chunk, 2)
        load(chunk).wait()
        for half in range(CHUNK // 16):
            for pair in range(rows // 2):
                block = [
                    stage[slot, pl.ds(16 * half, 16), 2 * pair + r].reshape(128, width)
                    for r in range(2)
                ]
                picked = jnp.dot(
                    select[...],
                    jnp.concatenate(block, axis=1),
                    preferred_element_type=F32,
                ).reshape(orb, 2, 8, 2 * width)
                picked = jnp.concatenate(
                    [picked[..., :width], picked[..., width:]], axis=2
                )
                send[chunk, :, pl.ds(2 * half, 2), pl.ds(16 * pair, 16), :] = (
                    picked.astype(BF16)
                )

        @pl.when(chunk + 2 < chunks)
        def _():
            load(chunk + 2).start()

    def own(chunk):
        return pltpu.make_async_copy(
            send.at[chunk, me], recv.at[chunk, :, me], own_sem.at[chunk]
        )

    def start(chunk):
        for step in range(1, orb):
            peer = orb_peer(step)
            pltpu.make_async_remote_copy(
                src_ref=send.at[chunk, peer],
                dst_ref=recv.at[chunk, :, me],
                send_sem=send_sem.at[chunk],
                recv_sem=recv_sem.at[chunk],
                device_id={"orb": peer},
                device_id_type=MESH,
            ).start()
        own(chunk).start()

    pack(0)
    pl.semaphore_wait(barrier, orb - 1 + jnp.minimum(my_z, 1) + my_core)
    start(0)
    for step in range(1, orb):
        pltpu.make_async_remote_copy(
            src_ref=occ_mine,
            dst_ref=occ_all.at[me],
            send_sem=small_send.at[0],
            recv_sem=small_recv.at[0],
            device_id={"orb": orb_peer(step)},
            device_id_type=MESH,
        ).start()
    def pack_and_start(chunk, carry):
        pack(chunk)
        start(chunk)
        return carry

    lax.fori_loop(1, chunks, pack_and_start, 0)

    def settle(ref, sem):
        pltpu.make_async_copy(ref, ref, sem).wait()

    settle(occ_all.at[pl.ds(0, orb - 1)], small_recv.at[0])

    @pl.when(my_core == 1)
    def _():
        pl.semaphore_signal(pair_sem, inc=1, device_id=at(my_z, 0), device_id_type=MESH)

    @pl.when(my_core == 0)
    def _():
        pl.semaphore_wait(pair_sem, 1)

    for sem, waits, sends, target in (
        (down_sem, my_z < planes - 1, my_z > 0, at(my_z - 1, my_core)),
        (up_sem, my_z > 0, my_z < planes - 1, at(my_z + 1, my_core)),
    ):

        @pl.when(waits)
        def _(sem=sem):
            pl.semaphore_wait(sem, 1)

        @pl.when(sends)
        def _(sem=sem, target=target):
            pl.semaphore_signal(sem, inc=1, device_id=target, device_id_type=MESH)

    for step in range(1, planes):
        pltpu.make_async_remote_copy(
            src_ref=gv_mine,
            dst_ref=gv_all.at[my_core, my_z],
            send_sem=small_send.at[1],
            recv_sem=small_recv.at[1],
            device_id=at(lax.rem(my_z + step, planes), my_core),
            device_id_type=MESH,
        ).start()
    settle(gv_all.at[0, pl.ds(0, planes - 1)], small_recv.at[1])
    swap = pltpu.make_async_remote_copy(
        src_ref=gv_all.at[my_core],
        dst_ref=gv_all.at[my_core],
        send_sem=small_send.at[2],
        recv_sem=small_recv.at[2],
        device_id=at(my_z, 1 - my_core),
        device_id_type=MESH,
    )
    swap.start()
    swap.wait()
    for t in range(2):
        for z in range(planes):
            for core in range(CORES):
                place = pl.ds((z * CORES + core) * rows, rows)
                gv_both[place, pl.ds(t * width, width)] = gv_all[core, z, t]

    deep = 8 * total_rows
    spread = (
        lax.broadcasted_iota(jnp.int32, (total_rows, deep), 1) // 8
        == lax.broadcasted_iota(jnp.int32, (total_rows, deep), 0)
    )
    spread = jnp.where(spread, 1.0, 0.0).astype(BF16)
    same = (
        lax.broadcasted_iota(jnp.int32, (16, 8, deep), 2) % 8
        == lax.broadcasted_iota(jnp.int32, (16, 8, deep), 1)
    )
    for t in range(2):

        def expand(pair, carry, t=t):
            two = occ_all[pl.ds(2 * pair, 2), t].reshape(2 * rows, width)
            wide = jnp.dot(two, spread, preferred_element_type=F32)
            wide = jnp.broadcast_to(wide[:, None, :], (16, 8, deep))
            wide = jnp.where(same, wide, 0.0).astype(BF16).reshape(128, deep)
            kron[pl.ds(pl.multiple_of((t * orb + 2 * pair) * 64, 128), 128), :] = wide
            return carry

        lax.fori_loop(0, orb // 2, expand, 0)

    def consume(chunk, carry):
        own(chunk).wait()
        settle(send.at[chunk, pl.ds(0, orb - 1)], recv_sem.at[chunk])
        for half in range(CHUNK // 16):
            first = chunk * CHUNK + 16 * half
            two = [recv[chunk, 2 * half + i].reshape(deep, width) for i in range(2)]
            place = pl.ds(pl.multiple_of(first, 16), 16)
            product = [
                jnp.dot(rows8, gv_both[...], preferred_element_type=F32).reshape(
                    total_rows, 8, 2 * width
                )
                for rows8 in two
            ]
            product = jnp.concatenate(product, axis=1).astype(BF16)
            virt[0, :, place, :] = product[..., :width]
            virt[1, :, place, :] = product[..., width:]
            both = jnp.concatenate(two, axis=1)
            for t in range(2):
                mixed = jnp.dot(
                    kron[pl.ds(t * deep, deep), :], both, preferred_element_type=F32
                ).reshape(total_rows, 8, 2 * width)
                mixed = jnp.concatenate([mixed[..., :width], mixed[..., width:]], axis=1)
                occp[t, :, place, :] = mixed.astype(BF16)
        return carry

    lax.fori_loop(0, chunks, consume, 0)

    many = 64
    for t in range(2):
        total[...] = jnp.zeros_like(total)

        def contract(block, carry, t=t):
            left = jnp.concatenate([occp[t, many * block + i] for i in range(many)], axis=1)
            right = jnp.concatenate([virt[t, many * block + i] for i in range(many)], axis=1)
            total[...] += lax.dot_general(
                left, right, (((1,), (1,)), ((), ())), preferred_element_type=F32
            )
            return carry

        lax.fori_loop(0, total_rows // many, contract, 0)
        term = (total[...] * tau_ref[t]).reshape(part.shape)
        part[...] = term if t == 0 else (part[...] + term) * scale

    for step in range(1, orb):
        peer = orb_peer(step)
        pltpu.make_async_remote_copy(
            src_ref=part.at[peer],
            dst_ref=shares.at[me],
            send_sem=share_send,
            recv_sem=share_recv,
            device_id={"orb": peer},
            device_id_type=MESH,
        ).start()
    shares[me] = part[me]
    settle(shares.at[pl.ds(0, orb - 1)], share_recv)
    whole = shares[0]
    for group in range(1, orb):
        whole = whole + shares[group]
    out_ref[...] = whole

    settle(shares.at[pl.ds(0, orb - 1)], share_send)
    settle(occ_all.at[pl.ds(0, orb - 1)], small_send.at[0])
    settle(gv_all.at[0, pl.ds(0, planes - 1)], small_send.at[1])

    def finish(chunk, carry):
        settle(send.at[chunk, pl.ds(0, orb - 1)], send_sem.at[chunk])
        return carry

    lax.fori_loop(0, chunks, finish, 0)


def on_device(b_rows, col_blocks, g_occ, occ_live, g_virt, tau_weight):
    orb, aux = lax.axis_size("orb"), lax.axis_size("aux")
    aux_dev, rows, slots, width = b_rows.shape
    chunks = aux_dev // CHUNK
    total_rows = orb * rows
    deep = 8 * total_rows
    scale = 1.0 / math.sqrt(total_rows * width * orb)
    smem = pl.BlockSpec(memory_space=pltpu.SMEM)
    vmem = pl.BlockSpec(memory_space=pltpu.VMEM)
    share = aux_dev // orb
    dma = pltpu.SemaphoreType.DMA
    return pl.pallas_call(
        functools.partial(kernel, orb, aux, math.isqrt(orb), scale),
        out_shape=jax.ShapeDtypeStruct((share, aux_dev), F32),
        in_specs=[smem, smem, smem, vmem, vmem, pl.BlockSpec(memory_space=pl.ANY)],
        out_specs=vmem,
        scratch_shapes=[
            pltpu.VMEM((2, CHUNK, rows, slots, width), BF16),
            pltpu.VMEM((chunks, orb, CHUNK // 8, 8 * rows, width), BF16),
            pltpu.VMEM((chunks, CHUNK // 8, orb, 8 * rows, width), BF16),
            pltpu.VMEM((2, total_rows, aux_dev, width), BF16),
            pltpu.VMEM((2, total_rows, aux_dev, width), BF16),
            pltpu.VMEM((2 * deep, deep), BF16),
            pltpu.VMEM((16 * orb, 128), BF16),
            pltpu.VMEM((2, rows, width), BF16),
            pltpu.VMEM((orb, 2, rows, width), BF16),
            pltpu.VMEM((2, rows, width), BF16),
            pltpu.VMEM((CORES, aux // CORES, 2, rows, width), BF16),
            pltpu.VMEM((width, 2 * width), BF16),
            pltpu.VMEM((aux_dev, aux_dev), F32),
            pltpu.VMEM((orb, share, aux_dev), F32),
            pltpu.VMEM((orb, share, aux_dev), F32),
            dma((2,)),
            dma((chunks,)),
            dma((chunks,)),
            dma((chunks,)),
            dma((3,)),
            dma((3,)),
            dma(()),
            dma(()),
            pltpu.SemaphoreType.REGULAR,
            pltpu.SemaphoreType.REGULAR,
            pltpu.SemaphoreType.REGULAR,
        ],
        compiler_params=pltpu.CompilerParams(
            collective_id=0, has_side_effects=True, vmem_limit_bytes=61 * 1024 * 1024
        ),
    )(col_blocks, occ_live, tau_weight, g_occ, g_virt, b_rows)


def solution(mesh):
    in_specs = (
        P("aux", "orb", None, None),
        P("orb", None),
        P(None, "orb", None),
        P(),
        P(None, "orb", "aux", None),
        P(),
    )
    out_specs = P("orb", "aux")
    return jax.shard_map(
        on_device, mesh=mesh, in_specs=in_specs, out_specs=out_specs, check_vma=False
    )
```

```python
import functools
import math

import jax
import jax.numpy as jnp
from jax import lax
from jax.experimental import pallas as pl
from jax.experimental.pallas import tpu as pltpu
from jax.sharding import PartitionSpec as P

MESH = pl.DeviceIdType.MESH
F32 = jnp.float32
BF16 = jnp.bfloat16
CHUNK = 16
CORES = 2


def kernel(
    orb,
    aux,
    side,
    scale,
    col_hbm,
    live_hbm,
    tau_hbm,
    occ_hbm,
    gv_hbm,
    b_ref,
    out_ref,
    col_ref,
    live_ref,
    tau_ref,
    occ_ref,
    stage,
    send,
    recv,
    virt,
    occp,
    kron,
    select,
    occ_mine,
    occ_all,
    gv_mine,
    gv_all,
    gv_both,
    total,
    part,
    shares,
    small_sem,
    stage_sem,
    own_sem,
    send_sem,
    recv_sem,
    small_send,
    small_recv,
    share_send,
    share_recv,
    pair_sem,
    down_sem,
    up_sem,
):
    me = lax.axis_index("orb")
    my_aux = lax.axis_index("aux")
    planes = aux // CORES
    my_z, my_core = my_aux // CORES, my_aux % CORES
    chunks = send.shape[0]
    rows = occ_ref.shape[1]
    total_rows = orb * rows
    width = occ_ref.shape[2]
    slots = col_ref.shape[1]
    my_y, my_x = me // side, me % side

    def orb_peer(step):
        step_y, step_x = step // side, step % side
        return lax.rem(my_y + step_y, side) * side + lax.rem(my_x + step_x, side)

    def at(z, core):
        return {"aux": z * CORES + core}

    def load(chunk):
        slot = lax.rem(chunk, 2)
        return pltpu.make_async_copy(
            b_ref.at[pl.ds(chunk * CHUNK, CHUNK)], stage.at[slot], stage_sem.at[slot]
        )

    def small(i):
        pairs = ((col_hbm, col_ref), (live_hbm, live_ref), (tau_hbm, tau_ref), (occ_hbm, occ_ref), (gv_hbm, gv_mine))
        return pltpu.make_async_copy(*pairs[i], small_sem.at[i])

    small(0).start()
    load(0).start()
    barrier = pltpu.get_barrier_semaphore()
    for step in range(1, orb):
        pl.semaphore_signal(
            barrier, inc=1, device_id={"orb": orb_peer(step)}, device_id_type=MESH
        )
    for ahead, target in ((my_z < planes - 1, at(my_z + 1, my_core)), (my_core == 0, at(my_z, 1))):

        @pl.when(ahead)
        def _(target=target):
            pl.semaphore_signal(barrier, inc=1, device_id=target, device_id_type=MESH)

    load(1).start()
    for i in range(1, 5):
        small(i).start()
    small(0).wait()

    lane = lax.broadcasted_iota(jnp.int32, (16 * orb, 128), 1)
    row = lax.broadcasted_iota(jnp.int32, (16 * orb, 128), 0)
    listed = jnp.zeros((16 * orb, 128), jnp.int32)
    for k in range(slots):
        listed = jnp.where(lane % slots == k, col_ref[0, k], listed)
    select[...] = jnp.where(
        (listed == row // 16) & (row % 16 == lane // slots), 1.0, 0.0
    ).astype(BF16)

    def pack(chunk):
        slot = lax.rem(chunk, 2)
        load(chunk).wait()
        for half in range(CHUNK // 16):
            for pair in range(rows // 2):
                block = [
                    stage[slot, pl.ds(16 * half, 16), 2 * pair + r].reshape(128, width)
                    for r in range(2)
                ]
                picked = jnp.dot(
                    select[...],
                    jnp.concatenate(block, axis=1),
                    preferred_element_type=F32,
                ).reshape(orb, 2, 8, 2 * width)
                picked = jnp.concatenate(
                    [picked[..., :width], picked[..., width:]], axis=2
                )
                send[chunk, :, pl.ds(2 * half, 2), pl.ds(16 * pair, 16), :] = (
                    picked.astype(BF16)
                )

        @pl.when(chunk + 2 < chunks)
        def _():
            load(chunk + 2).start()

    def own(chunk):
        return pltpu.make_async_copy(
            send.at[chunk, me], recv.at[chunk, :, me], own_sem.at[chunk]
        )

    def start(chunk):
        for step in range(1, orb):
            peer = orb_peer(step)
            pltpu.make_async_remote_copy(
                src_ref=send.at[chunk, peer],
                dst_ref=recv.at[chunk, :, me],
                send_sem=send_sem.at[chunk],
                recv_sem=recv_sem.at[chunk],
                device_id={"orb": peer},
                device_id_type=MESH,
            ).start()
        own(chunk).start()

    pack(0)
    pl.semaphore_wait(barrier, orb - 1 + jnp.minimum(my_z, 1) + my_core)
    start(0)
    for i in range(1, 5):
        small(i).wait()
    lane = lax.broadcasted_iota(jnp.int32, (rows, width), 1)
    for t in range(2):
        live = jnp.zeros((rows, width), jnp.int32)
        for group in range(orb):
            live = jnp.where(lane // rows == group, live_ref[t, me, group], live)
        occ_mine[t] = (occ_ref[t].astype(F32) * live.astype(F32)).astype(BF16)
    occ_all[me] = occ_mine[...]
    gv_all[my_core, my_z] = gv_mine[...]

    for step in range(1, orb):
        pltpu.make_async_remote_copy(
            src_ref=occ_mine,
            dst_ref=occ_all.at[me],
            send_sem=small_send.at[0],
            recv_sem=small_recv.at[0],
            device_id={"orb": orb_peer(step)},
            device_id_type=MESH,
        ).start()
    def pack_and_start(chunk, carry):
        pack(chunk)
        start(chunk)
        return carry

    lax.fori_loop(1, chunks, pack_and_start, 0)

    def settle(ref, sem):
        pltpu.make_async_copy(ref, ref, sem).wait()

    settle(occ_all.at[pl.ds(0, orb - 1)], small_recv.at[0])

    @pl.when(my_core == 1)
    def _():
        pl.semaphore_signal(pair_sem, inc=1, device_id=at(my_z, 0), device_id_type=MESH)

    @pl.when(my_core == 0)
    def _():
        pl.semaphore_wait(pair_sem, 1)

    for sem, waits, sends, target in (
        (down_sem, my_z < planes - 1, my_z > 0, at(my_z - 1, my_core)),
        (up_sem, my_z > 0, my_z < planes - 1, at(my_z + 1, my_core)),
    ):

        @pl.when(waits)
        def _(sem=sem):
            pl.semaphore_wait(sem, 1)

        @pl.when(sends)
        def _(sem=sem, target=target):
            pl.semaphore_signal(sem, inc=1, device_id=target, device_id_type=MESH)

    for step in range(1, planes):
        pltpu.make_async_remote_copy(
            src_ref=gv_mine,
            dst_ref=gv_all.at[my_core, my_z],
            send_sem=small_send.at[1],
            recv_sem=small_recv.at[1],
            device_id=at(lax.rem(my_z + step, planes), my_core),
            device_id_type=MESH,
        ).start()
    settle(gv_all.at[0, pl.ds(0, planes - 1)], small_recv.at[1])
    swap = pltpu.make_async_remote_copy(
        src_ref=gv_all.at[my_core],
        dst_ref=gv_all.at[my_core],
        send_sem=small_send.at[2],
        recv_sem=small_recv.at[2],
        device_id=at(my_z, 1 - my_core),
        device_id_type=MESH,
    )
    swap.start()
    swap.wait()
    for t in range(2):
        for z in range(planes):
            for core in range(CORES):
                place = pl.ds((z * CORES + core) * rows, rows)
                gv_both[place, pl.ds(t * width, width)] = gv_all[core, z, t, 0]

    deep = 8 * total_rows
    spread = (
        lax.broadcasted_iota(jnp.int32, (total_rows, deep), 1) // 8
        == lax.broadcasted_iota(jnp.int32, (total_rows, deep), 0)
    )
    spread = jnp.where(spread, 1.0, 0.0).astype(BF16)
    same = (
        lax.broadcasted_iota(jnp.int32, (16, 8, deep), 2) % 8
        == lax.broadcasted_iota(jnp.int32, (16, 8, deep), 1)
    )
    for t in range(2):

        def expand(pair, carry, t=t):
            two = occ_all[pl.ds(2 * pair, 2), t].reshape(2 * rows, width)
            wide = jnp.dot(two, spread, preferred_element_type=F32)
            wide = jnp.broadcast_to(wide[:, None, :], (16, 8, deep))
            wide = jnp.where(same, wide, 0.0).astype(BF16).reshape(128, deep)
            kron[pl.ds(pl.multiple_of((t * orb + 2 * pair) * 64, 128), 128), :] = wide
            return carry

        lax.fori_loop(0, orb // 2, expand, 0)

    def consume(chunk, carry):
        own(chunk).wait()
        settle(send.at[chunk, pl.ds(0, orb - 1)], recv_sem.at[chunk])
        for half in range(CHUNK // 16):
            first = chunk * CHUNK + 16 * half
            two = [recv[chunk, 2 * half + i].reshape(deep, width) for i in range(2)]
            place = pl.ds(pl.multiple_of(first, 16), 16)
            product = [
                jnp.dot(rows8, gv_both[...], preferred_element_type=F32).reshape(
                    total_rows, 8, 2 * width
                )
                for rows8 in two
            ]
            product = jnp.concatenate(product, axis=1).astype(BF16)
            virt[0, :, place, :] = product[..., :width]
            virt[1, :, place, :] = product[..., width:]
            both = jnp.concatenate(two, axis=1)
            for t in range(2):
                mixed = jnp.dot(
                    kron[pl.ds(t * deep, deep), :], both, preferred_element_type=F32
                ).reshape(total_rows, 8, 2 * width)
                mixed = jnp.concatenate([mixed[..., :width], mixed[..., width:]], axis=1)
                occp[t, :, place, :] = mixed.astype(BF16)
        return carry

    lax.fori_loop(0, chunks, consume, 0)

    for t in range(2):
        left = jnp.concatenate([occp[t, m] for m in range(total_rows)], axis=1)
        right = jnp.concatenate([virt[t, m] for m in range(total_rows)], axis=1)
        total[t] = lax.dot_general(
            left, right, (((1,), (1,)), ((), ())), preferred_element_type=F32
        ).reshape(part.shape)

    def weigh(peer):
        part[peer] = (total[0, peer] * tau_ref[0] + total[1, peer] * tau_ref[1]) * scale

    def hops(step):
        return sum(min(n, side - n) for n in (step // side, step % side))

    for step in sorted(range(1, orb), key=hops, reverse=True):
        peer = orb_peer(step)
        weigh(peer)
        pltpu.make_async_remote_copy(
            src_ref=part.at[peer],
            dst_ref=shares.at[me],
            send_sem=share_send,
            recv_sem=share_recv,
            device_id={"orb": peer},
            device_id_type=MESH,
        ).start()
    weigh(me)
    shares[me] = part[me]
    settle(shares.at[pl.ds(0, orb - 1)], share_recv)
    whole = shares[0]
    for group in range(1, orb):
        whole = whole + shares[group]
    out_ref[...] = whole

    settle(shares.at[pl.ds(0, orb - 1)], share_send)
    settle(occ_all.at[pl.ds(0, orb - 1)], small_send.at[0])
    settle(gv_all.at[0, pl.ds(0, planes - 1)], small_send.at[1])

    def finish(chunk, carry):
        settle(send.at[chunk, pl.ds(0, orb - 1)], send_sem.at[chunk])
        return carry

    lax.fori_loop(0, chunks, finish, 0)


def on_device(b_rows, col_blocks, g_occ, occ_live, g_virt, tau_weight):
    orb, aux = lax.axis_size("orb"), lax.axis_size("aux")
    aux_dev, rows, slots, width = b_rows.shape
    chunks = aux_dev // CHUNK
    total_rows = orb * rows
    deep = 8 * total_rows
    scale = 1.0 / math.sqrt(total_rows * width * orb)
    vmem = pl.BlockSpec(memory_space=pltpu.VMEM)
    share = aux_dev // orb
    dma = pltpu.SemaphoreType.DMA
    return pl.pallas_call(
        functools.partial(kernel, orb, aux, math.isqrt(orb), scale),
        out_shape=jax.ShapeDtypeStruct((share, aux_dev), F32),
        in_specs=[pl.BlockSpec(memory_space=pltpu.HBM)] * 6,
        out_specs=vmem,
        scratch_shapes=[
            pltpu.SMEM(col_blocks.shape, jnp.int32),
            pltpu.SMEM(occ_live.shape, jnp.int32),
            pltpu.SMEM(tau_weight.shape, F32),
            pltpu.VMEM(g_occ.shape, BF16),
            pltpu.VMEM((2, CHUNK, rows, slots, width), BF16),
            pltpu.VMEM((chunks, orb, CHUNK // 8, 8 * rows, width), BF16),
            pltpu.VMEM((chunks, CHUNK // 8, orb, 8 * rows, width), BF16),
            pltpu.VMEM((2, total_rows, aux_dev, width), BF16),
            pltpu.VMEM((2, total_rows, aux_dev, width), BF16),
            pltpu.VMEM((2 * deep, deep), BF16),
            pltpu.VMEM((16 * orb, 128), BF16),
            pltpu.VMEM((2, rows, width), BF16),
            pltpu.VMEM((orb, 2, rows, width), BF16),
            pltpu.VMEM(g_virt.shape, BF16),
            pltpu.VMEM((CORES, aux // CORES, *g_virt.shape), BF16),
            pltpu.VMEM((width, 2 * width), BF16),
            pltpu.VMEM((2, orb, share, aux_dev), F32),
            pltpu.VMEM((orb, share, aux_dev), F32),
            pltpu.VMEM((orb, share, aux_dev), F32),
            dma((5,)),
            dma((2,)),
            dma((chunks,)),
            dma((chunks,)),
            dma((chunks,)),
            dma((3,)),
            dma((3,)),
            dma(()),
            dma(()),
            pltpu.SemaphoreType.REGULAR,
            pltpu.SemaphoreType.REGULAR,
            pltpu.SemaphoreType.REGULAR,
        ],
        compiler_params=pltpu.CompilerParams(
            collective_id=0, has_side_effects=True, vmem_limit_bytes=61 * 1024 * 1024
        ),
    )(col_blocks, occ_live, tau_weight, g_occ, g_virt, b_rows)


def solution(mesh):
    in_specs = (
        P("aux", "orb", None, None),
        P("orb", None),
        P(None, "orb", None),
        P(),
        P(None, "orb", "aux", None),
        P(),
    )
    out_specs = P("orb", "aux")
    return jax.shard_map(
        on_device, mesh=mesh, in_specs=in_specs, out_specs=out_specs, check_vma=False
    )
```

```python
import functools
import math

import jax
import jax.numpy as jnp
from jax import lax
from jax.experimental import pallas as pl
from jax.experimental.pallas import tpu as pltpu
from jax.sharding import PartitionSpec as P

MESH = pl.DeviceIdType.MESH
F32 = jnp.float32
BF16 = jnp.bfloat16
CHUNK = 16
ORDER = [10, 1, 15, 4, 9, 3, 6, 12, 5, 11, 2, 14, 8, 7, 13]
CORES = 2


def kernel(
    orb,
    aux,
    side,
    scale,
    col_hbm,
    live_hbm,
    tau_hbm,
    occ_hbm,
    gv_hbm,
    b_ref,
    out_ref,
    col_ref,
    live_ref,
    tau_ref,
    occ_ref,
    stage,
    send,
    recv,
    virt,
    occp,
    kron,
    select,
    occ_mine,
    occ_all,
    gv_mine,
    gv_all,
    gv_both,
    total,
    part,
    shares,
    small_sem,
    stage_sem,
    own_sem,
    send_sem,
    recv_sem,
    small_send,
    small_recv,
    share_send,
    share_recv,
    pair_sem,
    down_sem,
    up_sem,
):
    me = lax.axis_index("orb")
    my_aux = lax.axis_index("aux")
    planes = aux // CORES
    my_z, my_core = my_aux // CORES, my_aux % CORES
    chunks = send.shape[0]
    rows = occ_ref.shape[1]
    total_rows = orb * rows
    width = occ_ref.shape[2]
    slots = col_ref.shape[1]
    my_y, my_x = me // side, me % side

    def orb_peer(step):
        step_y, step_x = step // side, step % side
        return lax.rem(my_y + step_y, side) * side + lax.rem(my_x + step_x, side)

    def at(z, core):
        return {"aux": z * CORES + core}

    def load(chunk):
        slot = lax.rem(chunk, 2)
        return pltpu.make_async_copy(
            b_ref.at[pl.ds(chunk * CHUNK, CHUNK)], stage.at[slot], stage_sem.at[slot]
        )

    def small(i):
        pairs = ((col_hbm, col_ref), (live_hbm, live_ref), (tau_hbm, tau_ref), (occ_hbm, occ_ref), (gv_hbm, gv_mine))
        return pltpu.make_async_copy(*pairs[i], small_sem.at[i])

    small(0).start()
    load(0).start()
    barrier = pltpu.get_barrier_semaphore()
    for step in range(1, orb):
        pl.semaphore_signal(
            barrier, inc=1, device_id={"orb": orb_peer(step)}, device_id_type=MESH
        )
    for ahead, target in ((my_z < planes - 1, at(my_z + 1, my_core)), (my_core == 0, at(my_z, 1))):

        @pl.when(ahead)
        def _(target=target):
            pl.semaphore_signal(barrier, inc=1, device_id=target, device_id_type=MESH)

    load(1).start()
    for i in range(1, 5):
        small(i).start()
    small(0).wait()

    lane = lax.broadcasted_iota(jnp.int32, (16 * orb, 128), 1)
    row = lax.broadcasted_iota(jnp.int32, (16 * orb, 128), 0)
    listed = jnp.zeros((16 * orb, 128), jnp.int32)
    for k in range(slots):
        listed = jnp.where(lane % slots == k, col_ref[0, k], listed)
    select[...] = jnp.where(
        (listed == row // 16) & (row % 16 == lane // slots), 1.0, 0.0
    ).astype(BF16)

    def pack(chunk):
        slot = lax.rem(chunk, 2)
        load(chunk).wait()
        for half in range(CHUNK // 16):
            for pair in range(rows // 2):
                block = [
                    stage[slot, pl.ds(16 * half, 16), 2 * pair + r].reshape(128, width)
                    for r in range(2)
                ]
                picked = jnp.dot(
                    select[...],
                    jnp.concatenate(block, axis=1),
                    preferred_element_type=F32,
                ).reshape(orb, 2, 8, 2 * width)
                picked = jnp.concatenate(
                    [picked[..., :width], picked[..., width:]], axis=2
                )
                send[chunk, :, pl.ds(2 * half, 2), pl.ds(16 * pair, 16), :] = (
                    picked.astype(BF16)
                )

        @pl.when(chunk + 2 < chunks)
        def _():
            load(chunk + 2).start()

    def own(chunk):
        return pltpu.make_async_copy(
            send.at[chunk, me], recv.at[chunk, :, me], own_sem.at[chunk]
        )

    def start(chunk):
        for step in ORDER:
            peer = orb_peer(step)
            pltpu.make_async_remote_copy(
                src_ref=send.at[chunk, peer],
                dst_ref=recv.at[chunk, :, me],
                send_sem=send_sem.at[chunk],
                recv_sem=recv_sem.at[chunk],
                device_id={"orb": peer},
                device_id_type=MESH,
            ).start()
        own(chunk).start()

    pack(0)
    pl.semaphore_wait(barrier, orb - 1 + jnp.minimum(my_z, 1) + my_core)
    start(0)
    for i in range(1, 5):
        small(i).wait()
    lane = lax.broadcasted_iota(jnp.int32, (rows, width), 1)
    for t in range(2):
        live = jnp.zeros((rows, width), jnp.int32)
        for group in range(orb):
            live = jnp.where(lane // rows == group, live_ref[t, me, group], live)
        occ_mine[t] = (occ_ref[t].astype(F32) * live.astype(F32)).astype(BF16)
    occ_all[me] = occ_mine[...]
    gv_all[my_core, my_z] = gv_mine[...]

    for step in range(1, orb):
        pltpu.make_async_remote_copy(
            src_ref=occ_mine,
            dst_ref=occ_all.at[me],
            send_sem=small_send.at[0],
            recv_sem=small_recv.at[0],
            device_id={"orb": orb_peer(step)},
            device_id_type=MESH,
        ).start()
    def pack_and_start(chunk, carry):
        pack(chunk)
        start(chunk)
        return carry

    lax.fori_loop(1, chunks, pack_and_start, 0)

    def settle(ref, sem):
        pltpu.make_async_copy(ref, ref, sem).wait()

    settle(occ_all.at[pl.ds(0, orb - 1)], small_recv.at[0])

    @pl.when(my_core == 1)
    def _():
        pl.semaphore_signal(pair_sem, inc=1, device_id=at(my_z, 0), device_id_type=MESH)

    @pl.when(my_core == 0)
    def _():
        pl.semaphore_wait(pair_sem, 1)

    for sem, waits, sends, target in (
        (down_sem, my_z < planes - 1, my_z > 0, at(my_z - 1, my_core)),
        (up_sem, my_z > 0, my_z < planes - 1, at(my_z + 1, my_core)),
    ):

        @pl.when(waits)
        def _(sem=sem):
            pl.semaphore_wait(sem, 1)

        @pl.when(sends)
        def _(sem=sem, target=target):
            pl.semaphore_signal(sem, inc=1, device_id=target, device_id_type=MESH)

    for step in range(1, planes):
        pltpu.make_async_remote_copy(
            src_ref=gv_mine,
            dst_ref=gv_all.at[my_core, my_z],
            send_sem=small_send.at[1],
            recv_sem=small_recv.at[1],
            device_id=at(lax.rem(my_z + step, planes), my_core),
            device_id_type=MESH,
        ).start()
    settle(gv_all.at[0, pl.ds(0, planes - 1)], small_recv.at[1])
    swap = pltpu.make_async_remote_copy(
        src_ref=gv_all.at[my_core],
        dst_ref=gv_all.at[my_core],
        send_sem=small_send.at[2],
        recv_sem=small_recv.at[2],
        device_id=at(my_z, 1 - my_core),
        device_id_type=MESH,
    )
    swap.start()
    swap.wait()
    for t in range(2):
        for z in range(planes):
            for core in range(CORES):
                place = pl.ds((z * CORES + core) * rows, rows)
                gv_both[place, pl.ds(t * width, width)] = gv_all[core, z, t, 0]

    deep = 8 * total_rows
    spread = (
        lax.broadcasted_iota(jnp.int32, (total_rows, deep), 1) // 8
        == lax.broadcasted_iota(jnp.int32, (total_rows, deep), 0)
    )
    spread = jnp.where(spread, 1.0, 0.0).astype(BF16)
    same = (
        lax.broadcasted_iota(jnp.int32, (16, 8, deep), 2) % 8
        == lax.broadcasted_iota(jnp.int32, (16, 8, deep), 1)
    )
    for t in range(2):

        def expand(pair, carry, t=t):
            two = occ_all[pl.ds(2 * pair, 2), t].reshape(2 * rows, width)
            wide = jnp.dot(two, spread, preferred_element_type=F32)
            wide = jnp.broadcast_to(wide[:, None, :], (16, 8, deep))
            wide = jnp.where(same, wide, 0.0).astype(BF16).reshape(128, deep)
            kron[pl.ds(pl.multiple_of((t * orb + 2 * pair) * 64, 128), 128), :] = wide
            return carry

        lax.fori_loop(0, orb // 2, expand, 0)

    def consume(chunk, carry):
        own(chunk).wait()
        settle(send.at[chunk, pl.ds(0, orb - 1)], recv_sem.at[chunk])
        for half in range(CHUNK // 16):
            first = chunk * CHUNK + 16 * half
            two = [recv[chunk, 2 * half + i].reshape(deep, width) for i in range(2)]
            place = pl.ds(pl.multiple_of(first, 16), 16)
            product = [
                jnp.dot(rows8, gv_both[...], preferred_element_type=F32).reshape(
                    total_rows, 8, 2 * width
                )
                for rows8 in two
            ]
            product = jnp.concatenate(product, axis=1).astype(BF16)
            virt[0, :, place, :] = product[..., :width]
            virt[1, :, place, :] = product[..., width:]
            both = jnp.concatenate(two, axis=1)
            for t in range(2):
                mixed = jnp.dot(
                    kron[pl.ds(t * deep, deep), :], both, preferred_element_type=F32
                ).reshape(total_rows, 8, 2 * width)
                mixed = jnp.concatenate([mixed[..., :width], mixed[..., width:]], axis=1)
                occp[t, :, place, :] = mixed.astype(BF16)
        return carry

    lax.fori_loop(0, chunks, consume, 0)

    for t in range(2):
        left = jnp.concatenate([occp[t, m] for m in range(total_rows)], axis=1)
        right = jnp.concatenate([virt[t, m] for m in range(total_rows)], axis=1)
        total[t] = lax.dot_general(
            left, right, (((1,), (1,)), ((), ())), preferred_element_type=F32
        ).reshape(part.shape)

    def weigh(peer):
        part[peer] = (total[0, peer] * tau_ref[0] + total[1, peer] * tau_ref[1]) * scale

    def hops(step):
        return sum(min(n, side - n) for n in (step // side, step % side))

    for step in sorted(range(1, orb), key=hops, reverse=True):
        peer = orb_peer(step)
        weigh(peer)
        pltpu.make_async_remote_copy(
            src_ref=part.at[peer],
            dst_ref=shares.at[me],
            send_sem=share_send,
            recv_sem=share_recv,
            device_id={"orb": peer},
            device_id_type=MESH,
        ).start()
    weigh(me)
    shares[me] = part[me]
    settle(shares.at[pl.ds(0, orb - 1)], share_recv)
    whole = shares[0]
    for group in range(1, orb):
        whole = whole + shares[group]
    out_ref[...] = whole

    settle(shares.at[pl.ds(0, orb - 1)], share_send)
    settle(occ_all.at[pl.ds(0, orb - 1)], small_send.at[0])
    settle(gv_all.at[0, pl.ds(0, planes - 1)], small_send.at[1])

    def finish(chunk, carry):
        settle(send.at[chunk, pl.ds(0, orb - 1)], send_sem.at[chunk])
        return carry

    lax.fori_loop(0, chunks, finish, 0)


def on_device(b_rows, col_blocks, g_occ, occ_live, g_virt, tau_weight):
    orb, aux = lax.axis_size("orb"), lax.axis_size("aux")
    aux_dev, rows, slots, width = b_rows.shape
    chunks = aux_dev // CHUNK
    total_rows = orb * rows
    deep = 8 * total_rows
    scale = 1.0 / math.sqrt(total_rows * width * orb)
    vmem = pl.BlockSpec(memory_space=pltpu.VMEM)
    share = aux_dev // orb
    dma = pltpu.SemaphoreType.DMA
    return pl.pallas_call(
        functools.partial(kernel, orb, aux, math.isqrt(orb), scale),
        out_shape=jax.ShapeDtypeStruct((share, aux_dev), F32),
        in_specs=[pl.BlockSpec(memory_space=pltpu.HBM)] * 6,
        out_specs=vmem,
        scratch_shapes=[
            pltpu.SMEM(col_blocks.shape, jnp.int32),
            pltpu.SMEM(occ_live.shape, jnp.int32),
            pltpu.SMEM(tau_weight.shape, F32),
            pltpu.VMEM(g_occ.shape, BF16),
            pltpu.VMEM((2, CHUNK, rows, slots, width), BF16),
            pltpu.VMEM((chunks, orb, CHUNK // 8, 8 * rows, width), BF16),
            pltpu.VMEM((chunks, CHUNK // 8, orb, 8 * rows, width), BF16),
            pltpu.VMEM((2, total_rows, aux_dev, width), BF16),
            pltpu.VMEM((2, total_rows, aux_dev, width), BF16),
            pltpu.VMEM((2 * deep, deep), BF16),
            pltpu.VMEM((16 * orb, 128), BF16),
            pltpu.VMEM((2, rows, width), BF16),
            pltpu.VMEM((orb, 2, rows, width), BF16),
            pltpu.VMEM(g_virt.shape, BF16),
            pltpu.VMEM((CORES, aux // CORES, *g_virt.shape), BF16),
            pltpu.VMEM((width, 2 * width), BF16),
            pltpu.VMEM((2, orb, share, aux_dev), F32),
            pltpu.VMEM((orb, share, aux_dev), F32),
            pltpu.VMEM((orb, share, aux_dev), F32),
            dma((5,)),
            dma((2,)),
            dma((chunks,)),
            dma((chunks,)),
            dma((chunks,)),
            dma((3,)),
            dma((3,)),
            dma(()),
            dma(()),
            pltpu.SemaphoreType.REGULAR,
            pltpu.SemaphoreType.REGULAR,
            pltpu.SemaphoreType.REGULAR,
        ],
        compiler_params=pltpu.CompilerParams(
            collective_id=0, has_side_effects=True, vmem_limit_bytes=61 * 1024 * 1024
        ),
    )(col_blocks, occ_live, tau_weight, g_occ, g_virt, b_rows)


def solution(mesh):
    in_specs = (
        P("aux", "orb", None, None),
        P("orb", None),
        P(None, "orb", None),
        P(),
        P(None, "orb", "aux", None),
        P(),
    )
    out_specs = P("orb", "aux")
    return jax.shard_map(
        on_device, mesh=mesh, in_specs=in_specs, out_specs=out_specs, check_vma=False
    )
```

```python
import functools
import math

import jax
import jax.numpy as jnp
from jax import lax
from jax.experimental import pallas as pl
from jax.experimental.pallas import tpu as pltpu
from jax.sharding import PartitionSpec as P

MESH = pl.DeviceIdType.MESH
F32 = jnp.float32
BF16 = jnp.bfloat16
CHUNK = 16
ORDER = [10, 1, 15, 4, 9, 3, 6, 12, 5, 11, 2, 14, 8, 7, 13]
CORES = 2


def kernel(
    orb,
    aux,
    side,
    scale,
    col_hbm,
    live_hbm,
    tau_hbm,
    occ_hbm,
    gv_hbm,
    b_ref,
    out_ref,
    col_ref,
    live_ref,
    tau_ref,
    occ_ref,
    stage,
    send,
    recv,
    virt,
    occp,
    kron,
    select,
    occ_mine,
    occ_all,
    gv_mine,
    gv_all,
    gv_both,
    total,
    part,
    shares,
    small_sem,
    stage_sem,
    own_sem,
    send_sem,
    recv_sem,
    small_send,
    small_recv,
    share_send,
    share_recv,
    pair_sem,
    down_sem,
    up_sem,
):
    me = lax.axis_index("orb")
    my_aux = lax.axis_index("aux")
    planes = aux // CORES
    my_z, my_core = my_aux // CORES, my_aux % CORES
    chunks = send.shape[0]
    rows = occ_ref.shape[1]
    total_rows = orb * rows
    width = occ_ref.shape[2]
    slots = col_ref.shape[1]
    my_y, my_x = me // side, me % side

    def orb_peer(step):
        step_y, step_x = step // side, step % side
        return lax.rem(my_y + step_y, side) * side + lax.rem(my_x + step_x, side)

    def at(z, core):
        return {"aux": z * CORES + core}

    def load(chunk):
        slot = lax.rem(chunk, 2)
        return pltpu.make_async_copy(
            b_ref.at[pl.ds(chunk * CHUNK, CHUNK)], stage.at[slot], stage_sem.at[slot]
        )

    def small(i):
        pairs = ((col_hbm, col_ref), (live_hbm, live_ref), (tau_hbm, tau_ref), (occ_hbm, occ_ref), (gv_hbm, gv_mine))
        return pltpu.make_async_copy(*pairs[i], small_sem.at[i])

    small(0).start()
    load(0).start()
    barrier = pltpu.get_barrier_semaphore()
    for step in range(1, orb):
        pl.semaphore_signal(
            barrier, inc=1, device_id={"orb": orb_peer(step)}, device_id_type=MESH
        )
    for ahead, target in ((my_z < planes - 1, at(my_z + 1, my_core)), (my_core == 0, at(my_z, 1))):

        @pl.when(ahead)
        def _(target=target):
            pl.semaphore_signal(barrier, inc=1, device_id=target, device_id_type=MESH)

    load(1).start()
    for i in range(1, 5):
        small(i).start()
    small(0).wait()

    lane = lax.broadcasted_iota(jnp.int32, (16 * orb, 128), 1)
    row = lax.broadcasted_iota(jnp.int32, (16 * orb, 128), 0)
    listed = jnp.zeros((16 * orb, 128), jnp.int32)
    for k in range(slots):
        listed = jnp.where(lane % slots == k, col_ref[0, k], listed)
    select[...] = jnp.where(
        (listed == row // 16) & (row % 16 == lane // slots), 1.0, 0.0
    ).astype(BF16)

    def pack(chunk):
        slot = lax.rem(chunk, 2)
        load(chunk).wait()
        for half in range(CHUNK // 16):
            for pair in range(rows // 2):
                block = [
                    stage[slot, pl.ds(16 * half, 16), 2 * pair + r].reshape(128, width)
                    for r in range(2)
                ]
                picked = jnp.dot(
                    select[...],
                    jnp.concatenate(block, axis=1),
                    preferred_element_type=F32,
                ).reshape(orb, 2, 8, 2 * width)
                picked = jnp.concatenate(
                    [picked[..., :width], picked[..., width:]], axis=2
                )
                send[chunk, :, pl.ds(2 * half, 2), pl.ds(16 * pair, 16), :] = (
                    picked.astype(BF16)
                )

        @pl.when(chunk + 2 < chunks)
        def _():
            load(chunk + 2).start()

    def own(chunk):
        return pltpu.make_async_copy(
            send.at[chunk, me], recv.at[chunk, :, me], own_sem.at[chunk]
        )

    def start(chunk):
        for step in ORDER:
            peer = orb_peer(step)
            pltpu.make_async_remote_copy(
                src_ref=send.at[chunk, peer],
                dst_ref=recv.at[chunk, :, me],
                send_sem=send_sem.at[chunk],
                recv_sem=recv_sem.at[chunk],
                device_id={"orb": peer},
                device_id_type=MESH,
            ).start()
        own(chunk).start()

    pack(0)
    pl.semaphore_wait(barrier, orb - 1 + jnp.minimum(my_z, 1) + my_core)
    start(0)
    for i in range(1, 5):
        small(i).wait()
    lane = lax.broadcasted_iota(jnp.int32, (rows, width), 1)
    for t in range(2):
        live = jnp.zeros((rows, width), jnp.int32)
        for group in range(orb):
            live = jnp.where(lane // rows == group, live_ref[t, me, group], live)
        occ_mine[t] = (occ_ref[t].astype(F32) * live.astype(F32)).astype(BF16)
    occ_all[me] = occ_mine[...]
    gv_all[my_core, my_z] = gv_mine[...]

    for step in range(1, orb):
        pltpu.make_async_remote_copy(
            src_ref=occ_mine,
            dst_ref=occ_all.at[me],
            send_sem=small_send.at[0],
            recv_sem=small_recv.at[0],
            device_id={"orb": orb_peer(step)},
            device_id_type=MESH,
        ).start()
    def pack_and_start(chunk, carry):
        pack(chunk)
        start(chunk)
        return carry

    lax.fori_loop(1, chunks, pack_and_start, 0)

    def settle(ref, sem):
        pltpu.make_async_copy(ref, ref, sem).wait()

    settle(occ_all.at[pl.ds(0, orb - 1)], small_recv.at[0])

    @pl.when(my_core == 1)
    def _():
        pl.semaphore_signal(pair_sem, inc=1, device_id=at(my_z, 0), device_id_type=MESH)

    @pl.when(my_core == 0)
    def _():
        pl.semaphore_wait(pair_sem, 1)

    for sem, waits, sends, target in (
        (down_sem, my_z < planes - 1, my_z > 0, at(my_z - 1, my_core)),
        (up_sem, my_z > 0, my_z < planes - 1, at(my_z + 1, my_core)),
    ):

        @pl.when(waits)
        def _(sem=sem):
            pl.semaphore_wait(sem, 1)

        @pl.when(sends)
        def _(sem=sem, target=target):
            pl.semaphore_signal(sem, inc=1, device_id=target, device_id_type=MESH)

    for step in range(1, planes):
        pltpu.make_async_remote_copy(
            src_ref=gv_mine,
            dst_ref=gv_all.at[my_core, my_z],
            send_sem=small_send.at[1],
            recv_sem=small_recv.at[1],
            device_id=at(lax.rem(my_z + step, planes), my_core),
            device_id_type=MESH,
        ).start()
    settle(gv_all.at[0, pl.ds(0, planes - 1)], small_recv.at[1])
    swap = pltpu.make_async_remote_copy(
        src_ref=gv_all.at[my_core],
        dst_ref=gv_all.at[my_core],
        send_sem=small_send.at[2],
        recv_sem=small_recv.at[2],
        device_id=at(my_z, 1 - my_core),
        device_id_type=MESH,
    )
    swap.start()
    swap.wait()
    for t in range(2):
        for z in range(planes):
            for core in range(CORES):
                place = pl.ds((z * CORES + core) * rows, rows)
                gv_both[place, pl.ds(t * width, width)] = gv_all[core, z, t, 0]

    deep = 8 * total_rows
    spread = (
        lax.broadcasted_iota(jnp.int32, (total_rows, deep), 1) // 8
        == lax.broadcasted_iota(jnp.int32, (total_rows, deep), 0)
    )
    spread = jnp.where(spread, 1.0, 0.0).astype(BF16)
    same = (
        lax.broadcasted_iota(jnp.int32, (16, 8, deep), 2) % 8
        == lax.broadcasted_iota(jnp.int32, (16, 8, deep), 1)
    )
    for t in range(2):

        def expand(pair, carry, t=t):
            two = occ_all[pl.ds(2 * pair, 2), t].reshape(2 * rows, width)
            wide = jnp.dot(two, spread, preferred_element_type=F32)
            wide = jnp.broadcast_to(wide[:, None, :], (16, 8, deep))
            wide = jnp.where(same, wide, 0.0).astype(BF16).reshape(128, deep)
            kron[pl.ds(pl.multiple_of((t * orb + 2 * pair) * 64, 128), 128), :] = wide
            return carry

        lax.fori_loop(0, orb // 2, expand, 0)

    def consume(chunk, carry):
        own(chunk).wait()
        settle(send.at[chunk, pl.ds(0, orb - 1)], recv_sem.at[chunk])
        for half in range(CHUNK // 16):
            first = chunk * CHUNK + 16 * half
            two = [recv[chunk, 2 * half + i].reshape(deep, width) for i in range(2)]
            place = pl.ds(pl.multiple_of(first, 16), 16)
            product = [
                jnp.dot(rows8, gv_both[...], preferred_element_type=F32).reshape(
                    total_rows, 8, 2 * width
                )
                for rows8 in two
            ]
            product = jnp.concatenate(product, axis=1).astype(BF16)
            virt[0, :, place, :] = product[..., :width]
            virt[1, :, place, :] = product[..., width:]
            both = jnp.concatenate(two, axis=1)
            mixed = jnp.dot(kron[...], both, preferred_element_type=F32).reshape(
                2, total_rows, 8, 2 * width
            )
            mixed = jnp.concatenate([mixed[..., :width], mixed[..., width:]], axis=2)
            occp[:, :, place, :] = mixed.astype(BF16)
        return carry

    lax.fori_loop(0, chunks, consume, 0)

    for t in range(2):
        left = jnp.concatenate([occp[t, m] for m in range(total_rows)], axis=1)
        right = jnp.concatenate([virt[t, m] for m in range(total_rows)], axis=1)
        total[t] = lax.dot_general(
            left, right, (((1,), (1,)), ((), ())), preferred_element_type=F32
        ).reshape(part.shape)

    def weigh(peer):
        part[peer] = (total[0, peer] * tau_ref[0] + total[1, peer] * tau_ref[1]) * scale

    def hops(step):
        return sum(min(n, side - n) for n in (step // side, step % side))

    for step in sorted(range(1, orb), key=hops, reverse=True):
        peer = orb_peer(step)
        weigh(peer)
        pltpu.make_async_remote_copy(
            src_ref=part.at[peer],
            dst_ref=shares.at[me],
            send_sem=share_send,
            recv_sem=share_recv,
            device_id={"orb": peer},
            device_id_type=MESH,
        ).start()
    weigh(me)
    shares[me] = part[me]
    settle(shares.at[pl.ds(0, orb - 1)], share_recv)
    whole = shares[0]
    for group in range(1, orb):
        whole = whole + shares[group]
    out_ref[...] = whole

    settle(shares.at[pl.ds(0, orb - 1)], share_send)
    settle(occ_all.at[pl.ds(0, orb - 1)], small_send.at[0])
    settle(gv_all.at[0, pl.ds(0, planes - 1)], small_send.at[1])

    def finish(chunk, carry):
        settle(send.at[chunk, pl.ds(0, orb - 1)], send_sem.at[chunk])
        return carry

    lax.fori_loop(0, chunks, finish, 0)


def on_device(b_rows, col_blocks, g_occ, occ_live, g_virt, tau_weight):
    orb, aux = lax.axis_size("orb"), lax.axis_size("aux")
    aux_dev, rows, slots, width = b_rows.shape
    chunks = aux_dev // CHUNK
    total_rows = orb * rows
    deep = 8 * total_rows
    scale = 1.0 / math.sqrt(total_rows * width * orb)
    vmem = pl.BlockSpec(memory_space=pltpu.VMEM)
    share = aux_dev // orb
    dma = pltpu.SemaphoreType.DMA
    return pl.pallas_call(
        functools.partial(kernel, orb, aux, math.isqrt(orb), scale),
        out_shape=jax.ShapeDtypeStruct((share, aux_dev), F32),
        in_specs=[pl.BlockSpec(memory_space=pltpu.HBM)] * 6,
        out_specs=vmem,
        scratch_shapes=[
            pltpu.SMEM(col_blocks.shape, jnp.int32),
            pltpu.SMEM(occ_live.shape, jnp.int32),
            pltpu.SMEM(tau_weight.shape, F32),
            pltpu.VMEM(g_occ.shape, BF16),
            pltpu.VMEM((2, CHUNK, rows, slots, width), BF16),
            pltpu.VMEM((chunks, orb, CHUNK // 8, 8 * rows, width), BF16),
            pltpu.VMEM((chunks, CHUNK // 8, orb, 8 * rows, width), BF16),
            pltpu.VMEM((2, total_rows, aux_dev, width), BF16),
            pltpu.VMEM((2, total_rows, aux_dev, width), BF16),
            pltpu.VMEM((2 * deep, deep), BF16),
            pltpu.VMEM((16 * orb, 128), BF16),
            pltpu.VMEM((2, rows, width), BF16),
            pltpu.VMEM((orb, 2, rows, width), BF16),
            pltpu.VMEM(g_virt.shape, BF16),
            pltpu.VMEM((CORES, aux // CORES, *g_virt.shape), BF16),
            pltpu.VMEM((width, 2 * width), BF16),
            pltpu.VMEM((2, orb, share, aux_dev), F32),
            pltpu.VMEM((orb, share, aux_dev), F32),
            pltpu.VMEM((orb, share, aux_dev), F32),
            dma((5,)),
            dma((2,)),
            dma((chunks,)),
            dma((chunks,)),
            dma((chunks,)),
            dma((3,)),
            dma((3,)),
            dma(()),
            dma(()),
            pltpu.SemaphoreType.REGULAR,
            pltpu.SemaphoreType.REGULAR,
            pltpu.SemaphoreType.REGULAR,
        ],
        compiler_params=pltpu.CompilerParams(
            collective_id=0, has_side_effects=True, vmem_limit_bytes=61 * 1024 * 1024
        ),
    )(col_blocks, occ_live, tau_weight, g_occ, g_virt, b_rows)


def solution(mesh):
    in_specs = (
        P("aux", "orb", None, None),
        P("orb", None),
        P(None, "orb", None),
        P(),
        P(None, "orb", "aux", None),
        P(),
    )
    out_specs = P("orb", "aux")
    return jax.shard_map(
        on_device, mesh=mesh, in_specs=in_specs, out_specs=out_specs, check_vma=False
    )
```
